32 devices in a mesh: groups: 2 (over y), dp: 16 (over z, x, core).
Axes of the slice: x: 2, y: 2, z: 4, core: 2. Of those that a mesh axis runs over, the one named last changes fastest.
Arguments:
- queries: bfloat16 [96, 128, 2560], P(('groups', 'dp')), parts along dimension 0, may hold values from -50 to 50
- keys: bfloat16 [96, 128, 2560], P(('groups', 'dp')), parts along dimension 0, may hold values from -4 to 4
- values: bfloat16 [96, 128, 2560], P(('groups', 'dp')), parts along dimension 0, may hold values from -6 to 6
- counts: int32 [32], P(('groups', 'dp')), parts along dimension 0, may hold values from 1 to 3, as said below
- neighbours: int32 [96, 3], P(('groups', 'dp')), parts along dimension 0, may hold values from 0 to 5, as said below
- gate_table: float32 [50, 2560], replicated, may hold values from 1 to 8
- step: int32 [1], replicated, may hold values from 0 to 49
- out_weight: bfloat16 [2560, 5120], P(None, 'dp'), may hold values from -0.125 to 0.125
Outputs:
- mixed: bfloat16 [96, 128, 5120], P(('groups', 'dp')), parts along dimension 0
The draws below stay inside these ranges and needn't reach their ends.
There are 2 independent parts, one for each index of `groups`. The reference program is written for one: setup_inputs(seed, part) draws one part's arguments, and reference() takes and returns one part's arrays. A program takes and returns all parts, laid end to end along the dimension named above; an argument that names none is the same for every part. Nothing has to cross between parts.
Inputs may be any that keep to these rules, and one draw needn't show every extreme that they name: `counts`: the live slots of a device come first. Member m holds the devices (m*4 + 4//2 + r) modulo the number of devices, r = 0 to 3, its tile list running through them in that order. Some device holds 3 live tiles. `neighbours`: row t (a tile of device d) names 3 places of device d's extended list: places 0 to 0 are tiles s to s+1 - 1 of device d-1 (around the axis) with s = max(counts[d-1]-1, 0), place 1+j is the device's slot j, places 1 + 3 onward are the first tiles of device d+1 (around the axis), and 5 names no tile. In a live tile's row the first entry is the tile itself and the others name distinct live tiles of the same member or no tile; rows of slots past the device's count name no tile at all.
All inputs are finite; a program needn't handle non-finite values.
Results may differ from the reference program's by a relative error of at most 0.0052.
Values may be sent and summed in bfloat16 or wider, within the bound.
A program may use at most 192 MiB of HBM per device.

```python
import math
import jax
import jax.numpy as jnp
from jax import lax

D = 5120
HEADS = 20
HEAD_DIM = 128
TILE = 128
HALO = 1
MEMBER_DEVS = 4
STEPS = 50
SLOTS = 3
NB = 3
TILES = 48


def member_layout():
    device_total = TILES // SLOTS
    member_total = device_total // MEMBER_DEVS
    device_ids = jnp.arange(device_total)
    relative = (device_ids - MEMBER_DEVS // 2) % device_total
    member_of = relative // MEMBER_DEVS
    rank_in = relative % MEMBER_DEVS
    member_devices = (jnp.arange(member_total)[:, None] * MEMBER_DEVS + MEMBER_DEVS // 2 + jnp.arange(MEMBER_DEVS)[None, :]) % device_total
    return (member_of, rank_in, member_devices)


def layout_counts(key):
    device_total = TILES // SLOTS
    member_total = device_total // MEMBER_DEVS
    member_of, rank_in, member_devices = member_layout()
    key_level, key_top, key_jitter, key_mask = jax.random.split(jax.random.fold_in(key, 101), 4)
    levels = jax.random.randint(key_level, (member_total,), 1, SLOTS + 1)
    busiest = jax.random.randint(key_top, (), 0, member_total)
    levels = jnp.where(jnp.arange(member_total) == busiest, SLOTS, levels)
    jitter = jax.random.randint(key_jitter, (device_total,), -1, 2)
    counts = jnp.clip(levels[member_of] + jitter, 1, SLOTS)
    busiest_device = (busiest * MEMBER_DEVS + MEMBER_DEVS // 2) % device_total
    counts = jnp.where(jnp.arange(device_total) == busiest_device, SLOTS, counts)
    return (counts.astype(jnp.int32), key_mask)


def draw_counts(key, part):
    return layout_counts(key)[0]


def draw_neighbours(key, part):
    counts, key_mask = layout_counts(key)
    device_total = TILES // SLOTS
    member_of, rank_in, member_devices = member_layout()
    member_counts = counts[member_devices]
    prefix = jnp.cumsum(member_counts, axis=1) - member_counts
    totals = jnp.sum(member_counts, axis=1)
    slot_ids = jnp.arange(SLOTS)
    member_prefix = prefix[member_of]
    own_prefix = jnp.take_along_axis(member_prefix, rank_in[:, None], axis=1)
    position = own_prefix + slot_ids[None, :]
    live = slot_ids[None, :] < counts[:, None]
    sentinel = SLOTS + 2 * HALO
    member_totals = totals[member_of][:, None]
    counts_before = jnp.roll(counts, 1)
    start_before = jnp.maximum(counts_before - HALO, 0)[:, None]
    columns = [jnp.where(live, HALO + slot_ids[None, :], sentinel)]
    for offset in range(-HALO, HALO + 1):
        if offset == 0:
            continue
        target = position + offset
        inside = (target >= 0) & (target < member_totals)
        target_rank = jnp.sum(member_prefix[:, None, :] <= target[:, :, None], axis=2) - 1
        target_rank = jnp.clip(target_rank, 0, MEMBER_DEVS - 1)
        target_slot = target - jnp.take_along_axis(member_prefix, target_rank, axis=1)
        delta = target_rank - rank_in[:, None]
        place = jnp.where(delta == 0, HALO + target_slot, jnp.where(delta == -1, target_slot - start_before, HALO + SLOTS + target_slot))
        present = jax.random.randint(jax.random.fold_in(key_mask, offset + 10), (device_total, SLOTS), 0, 4) != 0
        if offset < 0:
            forced = slot_ids[None, :] == 0
        else:
            forced = slot_ids[None, :] == counts[:, None] - 1
        keep = live & inside & (jnp.abs(delta) <= 1) & (present | forced)
        columns.append(jnp.where(keep, place, sentinel))
    table = jnp.stack(columns, axis=2)
    return table.reshape(TILES, -1).astype(jnp.int32)


def queries_and_keys(key):
    key_query, key_key = jax.random.split(jax.random.fold_in(key, 202))
    channels = HEADS * HEAD_DIM
    full_shape = (TILES, TILE, channels)
    keys_raw = jnp.clip(jax.random.normal(key_key, full_shape, jnp.float32), -4.0, 4.0)
    queries_raw = 2.5 * jnp.clip(jax.random.normal(key_query, full_shape, jnp.float32), -4.0, 4.0)
    queries_raw = jnp.clip(queries_raw, -50.0, 50.0)
    return (queries_raw, keys_raw)


def draw_queries(key, part):
    return queries_and_keys(key)[0].astype(jnp.bfloat16)


def draw_keys(key, part):
    return queries_and_keys(key)[1].astype(jnp.bfloat16)


def level_of(stream_key, shape, cuts, smallest, high):
    def one(axis_at, shards_of):
        draws = jax.random.uniform(jax.random.fold_in(jax.random.fold_in(stream_key, 6), axis_at), (shards_of,), jnp.float32, smallest / len(cuts), high / len(cuts))
        return jnp.repeat(jnp.exp(draws), shape[axis_at] // shards_of).reshape((-1,) + (1,) * (len(shape) - axis_at - 1))

    gain = one(*cuts[0])
    for cut in cuts[1:]:
        gain = gain * one(*cut)
    return gain


def gaussian(key, shape, deviation, bound, cuts=(), kind=jnp.bfloat16):
    values = jax.random.normal(key, shape, jnp.float32) * deviation
    if len(cuts) > 0:
        values = level_of(key, shape, cuts, -0.22, 0.18) * values
    return jnp.clip(values, min=-bound, max=bound).astype(kind)


def setup_inputs(seed: int = 0, part: int = 0) -> dict:
    arg_keys = jax.random.split(jax.random.key(seed), 9)
    own_keys = jax.random.split(jax.random.fold_in(arg_keys[8], part), 9)
    queries = draw_queries(jax.random.fold_in(jax.random.fold_in(arg_keys[8], part), 71), part)
    keys = draw_keys(jax.random.fold_in(jax.random.fold_in(arg_keys[8], part), 71), part)
    values = gaussian(own_keys[2], (TILES, TILE, HEADS * HEAD_DIM), 1.0, 6.0, ((0, 16),))
    counts = draw_counts(jax.random.fold_in(jax.random.fold_in(arg_keys[8], part), 71), part)
    neighbours = draw_neighbours(jax.random.fold_in(jax.random.fold_in(arg_keys[8], part), 71), part)
    gate_table = jnp.clip(jnp.exp(jax.random.uniform(arg_keys[5], (STEPS, HEADS * HEAD_DIM), jnp.float32, math.log(1.0), math.log(8.0))), 1.0, 8.0)
    step = jax.random.randint(arg_keys[6], (1,), 0, STEPS).astype(jnp.int32)
    out_weight = gaussian(arg_keys[7], (HEADS * HEAD_DIM, D), (HEADS * HEAD_DIM) ** -0.5, 0.125, ((1, 16),))
    return dict(queries=queries, keys=keys, values=values, counts=counts, neighbours=neighbours, gate_table=gate_table, step=step, out_weight=out_weight)


masked_score = -1e+30

def attend_tile(query_tile, key_rows, value_rows, key_valid, gate_row):
    query_rows = query_tile.shape[0]
    queries_h = query_tile.astype(jnp.float32).reshape(query_rows, HEADS, HEAD_DIM)
    keys_h = key_rows.astype(jnp.float32).reshape(-1, HEADS, HEAD_DIM)
    values_h = value_rows.astype(jnp.float32).reshape(-1, HEADS, HEAD_DIM)
    scores = jnp.einsum('qhd,khd->hqk', queries_h, keys_h) * (1.0 / math.sqrt(HEAD_DIM))
    scores = jnp.where(key_valid[None, None, :], scores, masked_score)
    row_max = lax.optimization_barrier(jnp.max(scores, axis=-1, keepdims=True))
    raw_weights = jnp.exp(scores - row_max)
    denominator = lax.optimization_barrier(jnp.sum(raw_weights, axis=-1))
    weights = lax.optimization_barrier(raw_weights.astype(jnp.bfloat16)).astype(jnp.float32)
    summed = jnp.einsum('hqk,khd->qhd', weights, values_h)
    summed = summed / jnp.transpose(denominator)[:, :, None]
    return (summed.reshape(query_rows, HEADS * HEAD_DIM) * gate_row[None, :]).astype(jnp.bfloat16)

def reference(queries, keys, values, counts, neighbours, gate_table, step, out_weight):
    channels = HEADS * HEAD_DIM
    device_total = TILES // SLOTS
    block_shape = (device_total, SLOTS, TILE, channels)
    key_blocks = keys.reshape(block_shape)
    value_blocks = values.reshape(block_shape)
    padded_keys = jnp.concatenate([key_blocks[-1:], key_blocks, key_blocks[:1]], axis=0)
    padded_values = jnp.concatenate([value_blocks[-1:], value_blocks, value_blocks[:1]], axis=0)
    counts_int = counts.astype(jnp.int32)
    padded_counts = jnp.concatenate([counts_int[-1:], counts_int, counts_int[:1]])
    query_blocks = queries.reshape(block_shape)
    index_blocks = neighbours.astype(jnp.int32).reshape(device_total, SLOTS, NB)
    gate_row = lax.dynamic_index_in_dim(gate_table, step[0].astype(jnp.int32), 0, keepdims=False)
    zero_tile = jnp.zeros((1, TILE, channels), keys.dtype)
    sentinel = SLOTS + 2 * HALO

    def extend(padded, device, start):
        before = lax.dynamic_slice_in_dim(lax.dynamic_index_in_dim(padded, device, 0, keepdims=False), start, HALO, 0)
        own_tiles = lax.dynamic_index_in_dim(padded, device + 1, 0, keepdims=False)
        after = lax.dynamic_index_in_dim(padded, device + 2, 0, keepdims=False)[:HALO]
        return jnp.concatenate([before, own_tiles, after, zero_tile], axis=0)

    def per_device(device):
        start = jnp.maximum(padded_counts[device] - HALO, 0).astype(jnp.int32)
        ext_keys = extend(padded_keys, device, start)
        ext_values = extend(padded_values, device, start)
        device_queries = lax.dynamic_index_in_dim(query_blocks, device, 0, keepdims=False)
        device_index = lax.dynamic_index_in_dim(index_blocks, device, 0, keepdims=False)
        live_count = padded_counts[device + 1]

        def per_slot(slot_id):
            tile_index = lax.dynamic_index_in_dim(device_index, slot_id, 0, keepdims=False)
            picked_keys = jnp.take(ext_keys, tile_index, axis=0).reshape(-1, channels)
            picked_values = jnp.take(ext_values, tile_index, axis=0).reshape(-1, channels)
            key_valid = jnp.repeat(tile_index != sentinel, TILE)
            query_tile = lax.dynamic_index_in_dim(device_queries, slot_id, 0, keepdims=False)
            computed = attend_tile(query_tile, picked_keys, picked_values, key_valid, gate_row)
            return jnp.where(slot_id < live_count, computed, jnp.zeros_like(computed))
        attended = lax.map(per_slot, jnp.arange(SLOTS, dtype=jnp.int32))
        projected = jnp.dot(attended.reshape(SLOTS * TILE, channels), out_weight, preferred_element_type=jnp.float32)
        return projected.astype(jnp.bfloat16).reshape(SLOTS, TILE, D)
    result = lax.map(per_device, jnp.arange(device_total, dtype=jnp.int32))
    return result.reshape(TILES, TILE, D)
```

```python
import functools
import math

import jax
import jax.numpy as jnp
from jax import lax
from jax.experimental import pallas as pl
from jax.experimental.pallas import tpu as pltpu
from jax.sharding import PartitionSpec as P

HEADS = 20
HALO = 1


masked_score = -1e30


def shifted(shard, axis, by):
    devices = lax.axis_size(axis)
    return lax.ppermute(shard, axis, [(i, (i + by) % devices) for i in range(devices)])


def attend_tile(query_tile, key_rows, value_rows, key_valid, gate_row):
    query_rows, channels = query_tile.shape
    head_dim = channels // HEADS
    queries_h = query_tile.reshape(query_rows, HEADS, head_dim)
    keys_h = key_rows.reshape(-1, HEADS, head_dim)
    values_h = value_rows.reshape(-1, HEADS, head_dim)
    scores = jnp.einsum("qhd,khd->hqk", queries_h, keys_h, preferred_element_type=jnp.float32) * (
        1.0 / math.sqrt(head_dim)
    )
    scores = jnp.where(key_valid[None, None, :], scores, masked_score)
    row_max = jnp.max(scores, axis=-1, keepdims=True)
    raw_weights = jnp.exp(scores - row_max)
    denominator = jnp.sum(raw_weights, axis=-1)
    weights = raw_weights.astype(jnp.bfloat16)
    summed = jnp.einsum("hqk,khd->qhd", weights, values_h, preferred_element_type=jnp.float32)
    summed = summed / jnp.transpose(denominator)[:, :, None]
    return (summed.reshape(query_rows, channels) * gate_row[None, :]).astype(jnp.bfloat16)


def on_device(queries, keys, values, counts, neighbours, gate_table, step, out_weight):
    slot_count, tile_rows, channels = queries.shape
    sentinel = slot_count + 2 * HALO
    own_count = counts[0]
    tail_start = jnp.maximum(own_count - HALO, 0)
    tail_block = jnp.stack(
        [
            lax.dynamic_slice_in_dim(keys, tail_start, HALO, 0),
            lax.dynamic_slice_in_dim(values, tail_start, HALO, 0),
        ]
    )
    lead_block = jnp.stack([keys[:HALO], values[:HALO]])
    from_before = shifted(tail_block, "dp", 1)
    from_after = shifted(lead_block, "dp", -1)
    zero_tile = jnp.zeros((1, tile_rows, channels), jnp.bfloat16)
    ext_keys = jnp.concatenate([from_before[0], keys, from_after[0], zero_tile], axis=0)
    ext_values = jnp.concatenate([from_before[1], values, from_after[1], zero_tile], axis=0)
    gate_row = lax.dynamic_index_in_dim(gate_table, step[0], 0, keepdims=False)

    def own_tile(slot_id, result):
        tile_index = lax.dynamic_index_in_dim(neighbours, slot_id, 0, keepdims=False)
        picked_keys = jnp.take(ext_keys, tile_index, axis=0).reshape(-1, channels)
        picked_values = jnp.take(ext_values, tile_index, axis=0).reshape(-1, channels)
        key_valid = jnp.repeat(tile_index != sentinel, tile_rows)
        query_tile = lax.dynamic_index_in_dim(queries, slot_id, 0, keepdims=False)
        computed = attend_tile(query_tile, picked_keys, picked_values, key_valid, gate_row)
        return lax.dynamic_update_index_in_dim(result, computed, slot_id, 0)

    attended = lax.fori_loop(0, own_count, own_tile, jnp.zeros_like(queries))
    flat_rows = attended.reshape(slot_count * tile_rows, channels)
    projected = jnp.dot(
        flat_rows,
        lax.all_gather(out_weight, "dp", axis=1, tiled=True),
        preferred_element_type=jnp.float32,
    )
    return projected.astype(jnp.bfloat16).reshape(slot_count, tile_rows, -1)


MESH = pl.DeviceIdType.MESH
NT = (((1,), (1,)), ((), ()))
UP, DOWN, ACROSS, OVER, PARTNER = range(5)


def fused(
    planes,
    keys_hbm,
    values_hbm,
    queries_hbm,
    tail_keys,
    tail_values,
    weight_hbm,
    gates_ref,
    bias_ref,
    places_ref,
    out_ref,
    ext_keys,
    ext_values,
    held_queries,
    attended,
    gathered,
    load_sem,
    halo_send,
    halo_recv,
    send_sem,
    class_recv,
    pair_recv,
):
    slots, rows, channels = held_queries.shape
    half = channels // 2
    head_dim = channels // HEADS
    devices = planes * 4
    group = lax.axis_index("groups")
    me = lax.axis_index("dp")
    core = lax.rem(me, 2)
    x = lax.rem(lax.div(me, 2), 2)
    z = lax.div(me, 4)
    after = lax.rem(me + 1, devices)
    before = lax.rem(me + devices - 1, devices)
    has_up = z < planes - 1
    has_down = z > 0
    targets = {
        UP: {"dp": me + 4},
        DOWN: {"dp": me - 4},
        ACROSS: {"dp": me + 2 - 4 * x},
        OVER: {"groups": 1 - group},
        PARTNER: {"dp": me + 1 - 2 * core},
    }

    loads = [
        pltpu.make_async_copy(weight_hbm.at[h], gathered.at[z * 2 + x, h, core], load_sem.at[h])
        for h in range(2)
    ]
    loads += [
        pltpu.make_async_copy(keys_hbm, ext_keys.at[pl.ds(HALO, slots)], load_sem.at[2]),
        pltpu.make_async_copy(values_hbm, ext_values.at[pl.ds(HALO, slots)], load_sem.at[3]),
        pltpu.make_async_copy(queries_hbm, held_queries, load_sem.at[4]),
    ]
    for load in loads:
        load.start()

    barrier = pltpu.get_barrier_semaphore()

    def greet(device):
        pl.semaphore_signal(barrier, inc=1, device_id=device, device_id_type=MESH)

    greet({"dp": after})
    greet({"dp": before})
    greet(targets[ACROSS])
    greet(targets[OVER])
    greet(targets[PARTNER])
    pl.when(has_up)(lambda: greet(targets[UP]))
    pl.when(has_down)(lambda: greet(targets[DOWN]))
    pl.semaphore_wait(barrier, 5 + has_up.astype(jnp.int32) + has_down.astype(jnp.int32))

    def halo(i, src, dst, device):
        return pltpu.make_async_remote_copy(
            src_ref=src,
            dst_ref=dst,
            send_sem=halo_send.at[i],
            recv_sem=halo_recv.at[i],
            device_id={"dp": device},
            device_id_type=MESH,
        )

    halos = [
        halo(0, tail_keys, ext_keys.at[pl.ds(0, HALO)], after),
        halo(1, keys_hbm.at[pl.ds(0, HALO)], ext_keys.at[pl.ds(HALO + slots, HALO)], before),
        halo(2, tail_values, ext_values.at[pl.ds(0, HALO)], after),
        halo(3, values_hbm.at[pl.ds(0, HALO)], ext_values.at[pl.ds(HALO + slots, HALO)], before),
    ]
    for copy in halos:
        copy.start()

    def hop(route, chip, h):
        piece = gathered.at[chip, h, core]
        recv = pair_recv if route == PARTNER else class_recv
        return pltpu.make_async_remote_copy(
            src_ref=piece,
            dst_ref=piece,
            send_sem=send_sem.at[route, chip, h],
            recv_sem=recv.at[chip, h],
            device_id=targets[route],
            device_id_type=MESH,
        )

    def arrive(chip, h):
        hop(ACROSS, chip, h).wait_recv()

    def arrive_pair(chip, h):
        piece = gathered.at[chip, h, 1 - core]
        pltpu.make_async_remote_copy(
            src_ref=piece,
            dst_ref=piece,
            send_sem=send_sem.at[PARTNER, chip, h],
            recv_sem=pair_recv.at[chip, h],
            device_id=targets[PARTNER],
            device_id_type=MESH,
        ).wait_recv()

    def start(route, chip, h):
        hop(route, chip, h).start()

    def finish(route, chip, h):
        hop(route, chip, h).wait_send()

    def own_sends(act):
        chip = z * 2 + x
        pl.when(has_up)(lambda: act(UP, chip, group))
        pl.when(has_down)(lambda: act(DOWN, chip, group))
        act(ACROSS, chip, group)
        act(ACROSS, chip, 1 - group)
        act(PARTNER, chip, 0)
        act(PARTNER, chip, 1)

    def at_distance(distance, do):
        for sign in (-1, 1):
            plane = z + sign * distance
            exists = plane >= 0 if sign < 0 else plane < planes
            pl.when(exists)(functools.partial(do, plane, sign))

    def line_step(distance, first, act):
        def do(plane, sign):
            chip = plane * 2 + x
            if first:
                arrive(chip, group)
            if sign < 0:
                pl.when(has_up)(lambda: act(UP, chip, group))
            else:
                pl.when(has_down)(lambda: act(DOWN, chip, group))
            act(OVER, chip, group)
            act(ACROSS, chip, group)
            act(PARTNER, chip, group)

        at_distance(distance, do)

    def across_own(first, act):
        chip = z * 2 + 1 - x
        for h in (group, 1 - group):
            if first:
                arrive(chip, h)
            act(PARTNER, chip, h)

    def plane_step(distance, first, act):
        def do(plane, sign):
            far, near = plane * 2 + 1 - x, plane * 2 + x
            if first:
                arrive(far, group)
            act(OVER, far, group)
            act(PARTNER, far, group)
            if first:
                arrive(near, 1 - group)
            act(PARTNER, near, 1 - group)

        at_distance(distance, do)

    def corner_step(distance, first, act):
        def do(plane, sign):
            chip = plane * 2 + 1 - x
            if first:
                arrive(chip, 1 - group)
            act(PARTNER, chip, 1 - group)

        at_distance(distance, do)

    def attend(slot):
        def one_head(head, carry):
            lanes = pl.ds(pl.multiple_of(head * head_dim, head_dim), head_dim)
            query = held_queries[slot, :, lanes]
            scores = [
                lax.dot_general(
                    query,
                    ext_keys[places_ref[slot, j], :, lanes],
                    NT,
                    preferred_element_type=jnp.float32,
                )
                * (1.0 / math.sqrt(head_dim))
                + bias_ref[slot, j]
                for j in range(3)
            ]
            row_max = jnp.max(
                jnp.maximum(jnp.maximum(scores[0], scores[1]), scores[2]), axis=-1, keepdims=True
            )
            raw = [jnp.exp(s - row_max) for s in scores]
            denominator = jnp.sum(raw[0] + raw[1] + raw[2], axis=-1, keepdims=True)
            summed = sum(
                jnp.dot(
                    raw[j].astype(jnp.bfloat16),
                    ext_values[places_ref[slot, j], :, lanes],
                    preferred_element_type=jnp.float32,
                )
                for j in range(3)
            )
            scaled = summed / denominator * gates_ref[slot, :, lanes]
            attended[pl.ds(slot * rows, rows), lanes] = scaled.astype(jnp.bfloat16)
            return carry

        lax.fori_loop(0, HEADS, one_head, 0, unroll=2)

    def project(chip):
        for h in range(2):
            arrive_pair(chip, h)
        columns = 2 * gathered.shape[3]
        total = sum(
            lax.dot_general(
                attended[:, h * half : (h + 1) * half],
                gathered[chip, h].reshape(columns, half),
                NT,
                preferred_element_type=jnp.float32,
            )
            for h in range(2)
        )
        out_ref[:, pl.ds(pl.multiple_of(chip * columns, columns), columns)] = total.astype(
            out_ref.dtype
        )

    for load in loads[:2]:
        load.wait()
    own_sends(start)
    for load in loads[2:]:
        load.wait()
    line_step(1, True, start)
    across_own(True, start)
    for copy in halos:
        copy.wait_recv()
    attend(0)
    for distance in range(2, planes):
        line_step(distance, True, start)
        if distance < slots + 1:
            attend(distance - 1)
        plane_step(distance - 1, True, start)
    for slot in range(planes - 1, slots):
        attend(slot)
    plane_step(planes - 1, True, start)
    project(z * 2 + 1 - x)

    def near_unit(plane, carry):
        project(plane * 2 + x)
        return carry

    lax.fori_loop(0, planes, near_unit, 0)
    for distance in range(1, planes):
        corner_step(distance, True, start)

    def far_unit(i, carry):
        plane = lax.rem(z + i, planes)
        project(plane * 2 + 1 - x)
        return carry

    lax.fori_loop(1, planes, far_unit, 0)

    own_sends(finish)
    across_own(False, finish)
    for distance in range(1, planes):
        line_step(distance, False, finish)
        plane_step(distance, False, finish)
        corner_step(distance, False, finish)
    for copy in halos:
        copy.wait_send()


def fits(mesh):
    return mesh.shape["groups"] == 2 and mesh.shape["dp"] in (8, 16)


def on_device_fused(mesh, queries, keys, values, counts, neighbours, gate_table, step, out_weight):
    slots, rows, channels = queries.shape
    planes = mesh.shape["dp"] // 4
    columns = out_weight.shape[1]
    if 2 * columns % 128 or columns % 16:
        return on_device(queries, keys, values, counts, neighbours, gate_table, step, out_weight)
    sentinel = slots + 2 * HALO
    tail_start = jnp.maximum(counts[0] - HALO, 0)
    tail_keys = lax.dynamic_slice_in_dim(keys, tail_start, HALO, 0)
    tail_values = lax.dynamic_slice_in_dim(values, tail_start, HALO, 0)
    half = channels // 2
    weight = jnp.transpose(out_weight.reshape(2, half, columns), (0, 2, 1))
    gate_row = lax.dynamic_index_in_dim(gate_table, step[0], 0, keepdims=False)
    live = (jnp.arange(slots) < counts[0]).astype(jnp.float32)
    gates = live[:, None, None] * gate_row[None, None, :]
    bias = jnp.where(neighbours == sentinel, masked_score, 0.0).astype(jnp.float32)
    bias = jnp.broadcast_to(bias[:, :, None, None], (slots, neighbours.shape[1], 1, rows))
    places = jnp.minimum(neighbours, sentinel - 1)
    chips = planes * 2
    anywhere = pl.BlockSpec(memory_space=pl.ANY)
    vmem = pl.BlockSpec(memory_space=pltpu.VMEM)
    out = pl.pallas_call(
        functools.partial(fused, planes),
        out_shape=jax.ShapeDtypeStruct((slots * rows, chips * 2 * columns), jnp.bfloat16),
        in_specs=[anywhere] * 6 + [vmem, vmem, pl.BlockSpec(memory_space=pltpu.SMEM)],
        out_specs=vmem,
        scratch_shapes=[
            pltpu.VMEM((sentinel, rows, channels), jnp.bfloat16),
            pltpu.VMEM((sentinel, rows, channels), jnp.bfloat16),
            pltpu.VMEM((slots, rows, channels), jnp.bfloat16),
            pltpu.VMEM((slots * rows, channels), jnp.bfloat16),
            pltpu.VMEM((chips, 2, 2, columns, half), jnp.bfloat16),
            pltpu.SemaphoreType.DMA((5,)),
            pltpu.SemaphoreType.DMA((4,)),
            pltpu.SemaphoreType.DMA((4,)),
            pltpu.SemaphoreType.DMA((5, chips, 2)),
            pltpu.SemaphoreType.DMA((chips, 2)),
            pltpu.SemaphoreType.DMA((chips, 2)),
        ],
        compiler_params=pltpu.CompilerParams(
            collective_id=0, has_side_effects=True, vmem_limit_bytes=60 * 2**20
        ),
        name="fused",
    )(keys, values, queries, tail_keys, tail_values, weight, gates, bias, places)
    return out.reshape(slots, rows, -1)


def solution(mesh):
    placed = (
        P(("groups", "dp"), None, None),
        P(("groups", "dp"), None, None),
        P(("groups", "dp"), None, None),
        P(("groups", "dp")),
        P(("groups", "dp"), None),
        P(),
        P(),
        P(None, "dp"),
    )
    return jax.shard_map(
        functools.partial(on_device_fused, mesh) if fits(mesh) else on_device,
        mesh=mesh,
        in_specs=placed,
        out_specs=P(("groups", "dp"), None, None),
        check_vma=False,
    )
```

```python
import functools
import math

import jax
import jax.numpy as jnp
from jax import lax
from jax.experimental import pallas as pl
from jax.experimental.pallas import tpu as pltpu
from jax.sharding import PartitionSpec as P

HEADS = 20
HALO = 1


masked_score = -1e30


def shifted(shard, axis, by):
    devices = lax.axis_size(axis)
    return lax.ppermute(shard, axis, [(i, (i + by) % devices) for i in range(devices)])


def attend_tile(query_tile, key_rows, value_rows, key_valid, gate_row):
    query_rows, channels = query_tile.shape
    head_dim = channels // HEADS
    queries_h = query_tile.reshape(query_rows, HEADS, head_dim)
    keys_h = key_rows.reshape(-1, HEADS, head_dim)
    values_h = value_rows.reshape(-1, HEADS, head_dim)
    scores = jnp.einsum("qhd,khd->hqk", queries_h, keys_h, preferred_element_type=jnp.float32) * (
        1.0 / math.sqrt(head_dim)
    )
    scores = jnp.where(key_valid[None, None, :], scores, masked_score)
    row_max = jnp.max(scores, axis=-1, keepdims=True)
    raw_weights = jnp.exp(scores - row_max)
    denominator = jnp.sum(raw_weights, axis=-1)
    weights = raw_weights.astype(jnp.bfloat16)
    summed = jnp.einsum("hqk,khd->qhd", weights, values_h, preferred_element_type=jnp.float32)
    summed = summed / jnp.transpose(denominator)[:, :, None]
    return (summed.reshape(query_rows, channels) * gate_row[None, :]).astype(jnp.bfloat16)


def on_device(queries, keys, values, counts, neighbours, gate_table, step, out_weight):
    slot_count, tile_rows, channels = queries.shape
    sentinel = slot_count + 2 * HALO
    own_count = counts[0]
    tail_start = jnp.maximum(own_count - HALO, 0)
    tail_block = jnp.stack(
        [
            lax.dynamic_slice_in_dim(keys, tail_start, HALO, 0),
            lax.dynamic_slice_in_dim(values, tail_start, HALO, 0),
        ]
    )
    lead_block = jnp.stack([keys[:HALO], values[:HALO]])
    from_before = shifted(tail_block, "dp", 1)
    from_after = shifted(lead_block, "dp", -1)
    zero_tile = jnp.zeros((1, tile_rows, channels), jnp.bfloat16)
    ext_keys = jnp.concatenate([from_before[0], keys, from_after[0], zero_tile], axis=0)
    ext_values = jnp.concatenate([from_before[1], values, from_after[1], zero_tile], axis=0)
    gate_row = lax.dynamic_index_in_dim(gate_table, step[0], 0, keepdims=False)

    def own_tile(slot_id, result):
        tile_index = lax.dynamic_index_in_dim(neighbours, slot_id, 0, keepdims=False)
        picked_keys = jnp.take(ext_keys, tile_index, axis=0).reshape(-1, channels)
        picked_values = jnp.take(ext_values, tile_index, axis=0).reshape(-1, channels)
        key_valid = jnp.repeat(tile_index != sentinel, tile_rows)
        query_tile = lax.dynamic_index_in_dim(queries, slot_id, 0, keepdims=False)
        computed = attend_tile(query_tile, picked_keys, picked_values, key_valid, gate_row)
        return lax.dynamic_update_index_in_dim(result, computed, slot_id, 0)

    attended = lax.fori_loop(0, own_count, own_tile, jnp.zeros_like(queries))
    flat_rows = attended.reshape(slot_count * tile_rows, channels)
    projected = jnp.dot(
        flat_rows,
        lax.all_gather(out_weight, "dp", axis=1, tiled=True),
        preferred_element_type=jnp.float32,
    )
    return projected.astype(jnp.bfloat16).reshape(slot_count, tile_rows, -1)


MESH = pl.DeviceIdType.MESH
NT = (((1,), (1,)), ((), ()))
UP, DOWN, ACROSS, OVER, PARTNER = range(5)
PARTS = 2
RELAYED = 2
CORNER_OVER = 0


def fused(
    planes,
    keys_hbm,
    values_hbm,
    queries_hbm,
    tail_keys,
    tail_values,
    weight_hbm,
    gates_ref,
    bias_ref,
    places_ref,
    out_ref,
    ext_keys,
    ext_values,
    held_queries,
    attended,
    gathered,
    load_sem,
    halo_send,
    halo_recv,
    send_sem,
    class_recv,
    pair_recv,
):
    slots, rows, channels = held_queries.shape
    half = channels // 2
    head_dim = channels // HEADS
    devices = planes * 4
    group = lax.axis_index("groups")
    me = lax.axis_index("dp")
    core = lax.rem(me, 2)
    x = lax.rem(lax.div(me, 2), 2)
    z = lax.div(me, 4)
    after = lax.rem(me + 1, devices)
    before = lax.rem(me + devices - 1, devices)
    has_up = z < planes - 1
    has_down = z > 0
    targets = {
        UP: {"dp": me + 4},
        DOWN: {"dp": me - 4},
        ACROSS: {"dp": me + 2 - 4 * x},
        OVER: {"groups": 1 - group},
        PARTNER: {"dp": me + 1 - 2 * core},
    }

    loads = [
        pltpu.make_async_copy(weight_hbm.at[h], gathered.at[z * 2 + x, h, core], load_sem.at[h])
        for h in range(2)
    ]
    loads += [
        pltpu.make_async_copy(keys_hbm, ext_keys.at[pl.ds(HALO, slots)], load_sem.at[2]),
        pltpu.make_async_copy(values_hbm, ext_values.at[pl.ds(HALO, slots)], load_sem.at[3]),
        pltpu.make_async_copy(queries_hbm, held_queries, load_sem.at[4]),
    ]
    for load in loads:
        load.start()

    barrier = pltpu.get_barrier_semaphore()

    def greet(device):
        pl.semaphore_signal(barrier, inc=1, device_id=device, device_id_type=MESH)

    greet({"dp": after})
    greet({"dp": before})
    greet(targets[ACROSS])
    greet(targets[OVER])
    greet(targets[PARTNER])
    pl.when(has_up)(lambda: greet(targets[UP]))
    pl.when(has_down)(lambda: greet(targets[DOWN]))
    pl.semaphore_wait(barrier, 5 + has_up.astype(jnp.int32) + has_down.astype(jnp.int32))

    def halo(i, src, dst, device):
        return pltpu.make_async_remote_copy(
            src_ref=src,
            dst_ref=dst,
            send_sem=halo_send.at[i],
            recv_sem=halo_recv.at[i],
            device_id={"dp": device},
            device_id_type=MESH,
        )

    halos = [
        halo(0, tail_keys, ext_keys.at[pl.ds(0, HALO)], after),
        halo(1, keys_hbm.at[pl.ds(0, HALO)], ext_keys.at[pl.ds(HALO + slots, HALO)], before),
        halo(2, tail_values, ext_values.at[pl.ds(0, HALO)], after),
        halo(3, values_hbm.at[pl.ds(0, HALO)], ext_values.at[pl.ds(HALO + slots, HALO)], before),
    ]

    span = gathered.shape[3] // PARTS
    mate = z + 1 - 2 * lax.rem(z, 2)

    def hop(route, chip, h, s):
        piece = gathered.at[chip, h, core, pl.ds(s * span, span)]
        recv = pair_recv if route == PARTNER else class_recv
        return pltpu.make_async_remote_copy(
            src_ref=piece,
            dst_ref=piece,
            send_sem=send_sem.at[route, chip, h, s],
            recv_sem=recv.at[chip, h, s],
            device_id=targets[route],
            device_id_type=MESH,
        )

    def arrive(chip, h, s):
        hop(ACROSS, chip, h, s).wait_recv()

    def arrive_pair(chip, h, s):
        piece = gathered.at[chip, h, 1 - core, pl.ds(s * span, span)]
        pltpu.make_async_remote_copy(
            src_ref=piece,
            dst_ref=piece,
            send_sem=send_sem.at[PARTNER, chip, h, s],
            recv_sem=pair_recv.at[chip, h, s],
            device_id=targets[PARTNER],
            device_id_type=MESH,
        ).wait_recv()

    def start(route, chip, h, s):
        hop(route, chip, h, s).start()

    def finish(route, chip, h, s):
        hop(route, chip, h, s).wait_send()

    def own_line(act):
        chip = z * 2 + x
        for s in range(PARTS):
            pl.when(has_up)(lambda: act(UP, chip, group, s))
            pl.when(has_down)(lambda: act(DOWN, chip, group, s))
            act(ACROSS, chip, group, s)

    def own_rest(act):
        for s in range(PARTS):
            act(ACROSS, z * 2 + x, 1 - group, s)

    def own_pair(act):
        for h in range(2):
            for s in range(PARTS):
                act(PARTNER, z * 2 + x, h, s)

    def relay(h, s, act):
        chip = z * 2 + 1 - x
        pl.when(mate > z)(lambda: act(UP, chip, h, s))
        pl.when(mate < z)(lambda: act(DOWN, chip, h, s))

    def at_distance(distance, do):
        for sign in (-1, 1):
            plane = z + sign * distance
            exists = plane >= 0 if sign < 0 else plane < planes
            pl.when(exists)(functools.partial(do, plane, sign))

    def line_step(distance, first, act):
        for s in range(PARTS):

            def do(plane, sign):
                chip = plane * 2 + x
                if first:
                    arrive(chip, group, s)
                if sign < 0:
                    pl.when(has_up)(lambda: act(UP, chip, group, s))
                else:
                    pl.when(has_down)(lambda: act(DOWN, chip, group, s))
                act(OVER, chip, group, s)
                if s < RELAYED:
                    pl.when(plane != mate)(lambda: act(ACROSS, chip, group, s))
                else:
                    act(ACROSS, chip, group, s)
                act(PARTNER, chip, group, s)

            at_distance(distance, do)

    def across_own(first, act):
        for s in range(PARTS):
            if first:
                arrive(z * 2 + 1 - x, group, s)
            act(PARTNER, z * 2 + 1 - x, group, s)

    def relay_own(act):
        for s in range(RELAYED):
            relay(group, s, act)

    def across_rest(first, act):
        for s in range(PARTS):
            if first:
                arrive(z * 2 + 1 - x, 1 - group, s)
            if s >= CORNER_OVER:
                relay(1 - group, s, act)
            act(PARTNER, z * 2 + 1 - x, 1 - group, s)

    def near_step(distance, first, act):
        for s in range(PARTS):

            def do(plane, sign):
                if first:
                    arrive(plane * 2 + x, 1 - group, s)
                act(PARTNER, plane * 2 + x, 1 - group, s)

            at_distance(distance, do)

    def far_piece(chip, s, over, first, act):
        if first:
            arrive(chip, group, s)
        if over:
            act(OVER, chip, group, s)
        act(PARTNER, chip, group, s)

    def far_step(distance, first, act):
        for s in range(PARTS):

            def do(plane, sign):
                pl.when(plane != mate)(
                    lambda: far_piece(plane * 2 + 1 - x, s, True, first, act)
                )

            at_distance(distance, do)

    def mate_step(first, act):
        for s in range(PARTS):
            far_piece(mate * 2 + 1 - x, s, s < CORNER_OVER, first, act)

    def corner_step(distance, first, act):
        def do(plane, sign):
            chip = plane * 2 + 1 - x
            for s in range(PARTS):
                if first:
                    arrive(chip, 1 - group, s)
                act(PARTNER, chip, 1 - group, s)
            if first:
                project(chip)

        at_distance(distance, do)

    def attend(slot):
        def one_head(head, carry):
            lanes = pl.ds(pl.multiple_of(head * head_dim, head_dim), head_dim)
            query = held_queries[slot, :, lanes]
            scores = [
                lax.dot_general(
                    query,
                    ext_keys[places_ref[slot, j], :, lanes],
                    NT,
                    preferred_element_type=jnp.float32,
                )
                * (1.0 / math.sqrt(head_dim))
                + bias_ref[slot, j]
                for j in range(3)
            ]
            row_max = jnp.max(
                jnp.maximum(jnp.maximum(scores[0], scores[1]), scores[2]), axis=-1, keepdims=True
            )
            raw = [jnp.exp(s - row_max) for s in scores]
            denominator = jnp.sum(raw[0] + raw[1] + raw[2], axis=-1, keepdims=True)
            summed = sum(
                jnp.dot(
                    raw[j].astype(jnp.bfloat16),
                    ext_values[places_ref[slot, j], :, lanes],
                    preferred_element_type=jnp.float32,
                )
                for j in range(3)
            )
            scaled = summed / denominator * gates_ref[slot, :, lanes]
            attended[pl.ds(slot * rows, rows), lanes] = scaled.astype(jnp.bfloat16)
            return carry

        lax.fori_loop(0, HEADS, one_head, 0, unroll=2)

    def project(chip):
        for h in range(2):
            for s in range(PARTS):
                arrive_pair(chip, h, s)
        columns = 2 * gathered.shape[3]
        total = sum(
            lax.dot_general(
                attended[:, h * half : (h + 1) * half],
                gathered[chip, h].reshape(columns, half),
                NT,
                preferred_element_type=jnp.float32,
            )
            for h in range(2)
        )
        out_ref[:, pl.ds(pl.multiple_of(chip * columns, columns), columns)] = total.astype(
            out_ref.dtype
        )

    for load in loads[:2]:
        load.wait()
    edge = jnp.logical_or(z == 0, z == planes - 1)
    inner = jnp.logical_not(edge)
    own_line(start)
    for copy in halos:
        copy.start()
    own_pair(start)
    line_step(1, True, start)
    across_own(True, start)
    for load in loads[2:]:
        load.wait()
    for distance in range(2, planes):
        line_step(distance, True, start)
        if distance == 2:
            pl.when(inner)(lambda: own_rest(start))
            relay_own(start)
    pl.when(edge)(lambda: own_rest(start))
    if planes == 2:
        relay_own(start)
    for copy in halos:
        copy.wait_recv()
    attend(0)
    for distance in range(1, planes):
        near_step(distance, True, start)
        far_step(distance, True, start)
        if distance < slots:
            attend(distance)
    for slot in range(planes, slots):
        attend(slot)

    def near_unit(plane, carry):
        project(plane * 2 + x)
        return carry

    lax.fori_loop(0, planes, near_unit, 0)
    mate_step(True, start)
    across_rest(True, start)
    project(z * 2 + 1 - x)
    for distance in range(planes - 1, 0, -1):
        corner_step(distance, True, start)

    own_line(finish)
    own_rest(finish)
    own_pair(finish)
    across_own(False, finish)
    relay_own(finish)
    across_rest(False, finish)
    mate_step(False, finish)
    for distance in range(1, planes):
        line_step(distance, False, finish)
        near_step(distance, False, finish)
        far_step(distance, False, finish)
        corner_step(distance, False, finish)
    for copy in halos:
        copy.wait_send()


def fits(mesh):
    return mesh.shape["groups"] == 2 and mesh.shape["dp"] in (8, 16)


def on_device_fused(mesh, queries, keys, values, counts, neighbours, gate_table, step, out_weight):
    slots, rows, channels = queries.shape
    planes = mesh.shape["dp"] // 4
    columns = out_weight.shape[1]
    if 2 * columns % 128 or columns % (16 * PARTS):
        return on_device(queries, keys, values, counts, neighbours, gate_table, step, out_weight)
    sentinel = slots + 2 * HALO
    tail_start = jnp.maximum(counts[0] - HALO, 0)
    tail_keys = lax.dynamic_slice_in_dim(keys, tail_start, HALO, 0)
    tail_values = lax.dynamic_slice_in_dim(values, tail_start, HALO, 0)
    half = channels // 2
    weight = jnp.transpose(out_weight.reshape(2, half, columns), (0, 2, 1))
    gate_row = lax.dynamic_index_in_dim(gate_table, step[0], 0, keepdims=False)
    live = (jnp.arange(slots) < counts[0]).astype(jnp.float32)
    gates = live[:, None, None] * gate_row[None, None, :]
    bias = jnp.where(neighbours == sentinel, masked_score, 0.0).astype(jnp.float32)
    bias = jnp.broadcast_to(bias[:, :, None, None], (slots, neighbours.shape[1], 1, rows))
    places = jnp.minimum(neighbours, sentinel - 1)
    chips = planes * 2
    anywhere = pl.BlockSpec(memory_space=pl.ANY)
    vmem = pl.BlockSpec(memory_space=pltpu.VMEM)
    out = pl.pallas_call(
        functools.partial(fused, planes),
        out_shape=jax.ShapeDtypeStruct((slots * rows, chips * 2 * columns), jnp.bfloat16),
        in_specs=[anywhere] * 6 + [vmem, vmem, pl.BlockSpec(memory_space=pltpu.SMEM)],
        out_specs=vmem,
        scratch_shapes=[
            pltpu.VMEM((sentinel, rows, channels), jnp.bfloat16),
            pltpu.VMEM((sentinel, rows, channels), jnp.bfloat16),
            pltpu.VMEM((slots, rows, channels), jnp.bfloat16),
            pltpu.VMEM((slots * rows, channels), jnp.bfloat16),
            pltpu.VMEM((chips, 2, 2, columns, half), jnp.bfloat16),
            pltpu.SemaphoreType.DMA((5,)),
            pltpu.SemaphoreType.DMA((4,)),
            pltpu.SemaphoreType.DMA((4,)),
            pltpu.SemaphoreType.DMA((5, chips, 2, PARTS)),
            pltpu.SemaphoreType.DMA((chips, 2, PARTS)),
            pltpu.SemaphoreType.DMA((chips, 2, PARTS)),
        ],
        compiler_params=pltpu.CompilerParams(
            collective_id=0, has_side_effects=True, vmem_limit_bytes=60 * 2**20
        ),
        name="fused",
    )(keys, values, queries, tail_keys, tail_values, weight, gates, bias, places)
    return out.reshape(slots, rows, -1)


def solution(mesh):
    placed = (
        P(("groups", "dp"), None, None),
        P(("groups", "dp"), None, None),
        P(("groups", "dp"), None, None),
        P(("groups", "dp")),
        P(("groups", "dp"), None),
        P(),
        P(),
        P(None, "dp"),
    )
    return jax.shard_map(
        functools.partial(on_device_fused, mesh) if fits(mesh) else on_device,
        mesh=mesh,
        in_specs=placed,
        out_specs=P(("groups", "dp"), None, None),
        check_vma=False,
    )
```

```python
import functools
import math

import jax
import jax.numpy as jnp
from jax import lax
from jax.experimental import pallas as pl
from jax.experimental.pallas import tpu as pltpu
from jax.sharding import PartitionSpec as P

HEADS = 20
HALO = 1


masked_score = -1e30


def shifted(shard, axis, by):
    devices = lax.axis_size(axis)
    return lax.ppermute(shard, axis, [(i, (i + by) % devices) for i in range(devices)])


def attend_tile(query_tile, key_rows, value_rows, key_valid, gate_row):
    query_rows, channels = query_tile.shape
    head_dim = channels // HEADS
    queries_h = query_tile.reshape(query_rows, HEADS, head_dim)
    keys_h = key_rows.reshape(-1, HEADS, head_dim)
    values_h = value_rows.reshape(-1, HEADS, head_dim)
    scores = jnp.einsum("qhd,khd->hqk", queries_h, keys_h, preferred_element_type=jnp.float32) * (
        1.0 / math.sqrt(head_dim)
    )
    scores = jnp.where(key_valid[None, None, :], scores, masked_score)
    row_max = jnp.max(scores, axis=-1, keepdims=True)
    raw_weights = jnp.exp(scores - row_max)
    denominator = jnp.sum(raw_weights, axis=-1)
    weights = raw_weights.astype(jnp.bfloat16)
    summed = jnp.einsum("hqk,khd->qhd", weights, values_h, preferred_element_type=jnp.float32)
    summed = summed / jnp.transpose(denominator)[:, :, None]
    return (summed.reshape(query_rows, channels) * gate_row[None, :]).astype(jnp.bfloat16)


def on_device(queries, keys, values, counts, neighbours, gate_table, step, out_weight):
    slot_count, tile_rows, channels = queries.shape
    sentinel = slot_count + 2 * HALO
    own_count = counts[0]
    tail_start = jnp.maximum(own_count - HALO, 0)
    tail_block = jnp.stack(
        [
            lax.dynamic_slice_in_dim(keys, tail_start, HALO, 0),
            lax.dynamic_slice_in_dim(values, tail_start, HALO, 0),
        ]
    )
    lead_block = jnp.stack([keys[:HALO], values[:HALO]])
    from_before = shifted(tail_block, "dp", 1)
    from_after = shifted(lead_block, "dp", -1)
    zero_tile = jnp.zeros((1, tile_rows, channels), jnp.bfloat16)
    ext_keys = jnp.concatenate([from_before[0], keys, from_after[0], zero_tile], axis=0)
    ext_values = jnp.concatenate([from_before[1], values, from_after[1], zero_tile], axis=0)
    gate_row = lax.dynamic_index_in_dim(gate_table, step[0], 0, keepdims=False)

    def own_tile(slot_id, result):
        tile_index = lax.dynamic_index_in_dim(neighbours, slot_id, 0, keepdims=False)
        picked_keys = jnp.take(ext_keys, tile_index, axis=0).reshape(-1, channels)
        picked_values = jnp.take(ext_values, tile_index, axis=0).reshape(-1, channels)
        key_valid = jnp.repeat(tile_index != sentinel, tile_rows)
        query_tile = lax.dynamic_index_in_dim(queries, slot_id, 0, keepdims=False)
        computed = attend_tile(query_tile, picked_keys, picked_values, key_valid, gate_row)
        return lax.dynamic_update_index_in_dim(result, computed, slot_id, 0)

    attended = lax.fori_loop(0, own_count, own_tile, jnp.zeros_like(queries))
    flat_rows = attended.reshape(slot_count * tile_rows, channels)
    projected = jnp.dot(
        flat_rows,
        lax.all_gather(out_weight, "dp", axis=1, tiled=True),
        preferred_element_type=jnp.float32,
    )
    return projected.astype(jnp.bfloat16).reshape(slot_count, tile_rows, -1)


MESH = pl.DeviceIdType.MESH
NT = (((1,), (1,)), ((), ()))
UP, DOWN, ACROSS, OVER, PARTNER = range(5)
PARTS = 2
RELAYED = 2
CORNER_OVER = 0


def fused(
    planes,
    keys_hbm,
    values_hbm,
    queries_hbm,
    tail_keys,
    tail_values,
    weight_hbm,
    gates_ref,
    bias_ref,
    places_ref,
    out_ref,
    ext_keys,
    ext_values,
    held_queries,
    attended,
    gathered,
    load_sem,
    halo_send,
    halo_recv,
    send_sem,
    class_recv,
    pair_recv,
):
    slots, rows, channels = held_queries.shape
    half = channels // 2
    head_dim = channels // HEADS
    devices = planes * 4
    group = lax.axis_index("groups")
    me = lax.axis_index("dp")
    core = lax.rem(me, 2)
    x = lax.rem(lax.div(me, 2), 2)
    z = lax.div(me, 4)
    after = lax.rem(me + 1, devices)
    before = lax.rem(me + devices - 1, devices)
    has_up = z < planes - 1
    has_down = z > 0
    targets = {
        UP: {"dp": me + 4},
        DOWN: {"dp": me - 4},
        ACROSS: {"dp": me + 2 - 4 * x},
        OVER: {"groups": 1 - group},
        PARTNER: {"dp": me + 1 - 2 * core},
    }

    loads = [
        pltpu.make_async_copy(weight_hbm.at[h], gathered.at[z * 2 + x, h, core], load_sem.at[h])
        for h in range(2)
    ]
    loads += [
        pltpu.make_async_copy(keys_hbm, ext_keys.at[pl.ds(HALO, slots)], load_sem.at[2]),
        pltpu.make_async_copy(values_hbm, ext_values.at[pl.ds(HALO, slots)], load_sem.at[3]),
        pltpu.make_async_copy(queries_hbm, held_queries, load_sem.at[4]),
    ]
    for load in loads:
        load.start()

    barrier = pltpu.get_barrier_semaphore()

    def greet(device):
        pl.semaphore_signal(barrier, inc=1, device_id=device, device_id_type=MESH)

    greet({"dp": after})
    greet({"dp": before})
    greet(targets[ACROSS])
    greet(targets[OVER])
    greet(targets[PARTNER])
    pl.when(has_up)(lambda: greet(targets[UP]))
    pl.when(has_down)(lambda: greet(targets[DOWN]))
    pl.semaphore_wait(barrier, 5 + has_up.astype(jnp.int32) + has_down.astype(jnp.int32))

    def halo(i, src, dst, device):
        return pltpu.make_async_remote_copy(
            src_ref=src,
            dst_ref=dst,
            send_sem=halo_send.at[i],
            recv_sem=halo_recv.at[i],
            device_id={"dp": device},
            device_id_type=MESH,
        )

    halos = [
        halo(0, tail_keys, ext_keys.at[pl.ds(0, HALO)], after),
        halo(1, keys_hbm.at[pl.ds(0, HALO)], ext_keys.at[pl.ds(HALO + slots, HALO)], before),
        halo(2, tail_values, ext_values.at[pl.ds(0, HALO)], after),
        halo(3, values_hbm.at[pl.ds(0, HALO)], ext_values.at[pl.ds(HALO + slots, HALO)], before),
    ]

    span = gathered.shape[3] // PARTS
    mate = z + 1 - 2 * lax.rem(z, 2)

    def hop(route, chip, h, s):
        piece = gathered.at[chip, h, core, pl.ds(s * span, span)]
        recv = pair_recv if route == PARTNER else class_recv
        return pltpu.make_async_remote_copy(
            src_ref=piece,
            dst_ref=piece,
            send_sem=send_sem.at[route, chip, h, s],
            recv_sem=recv.at[chip, h, s],
            device_id=targets[route],
            device_id_type=MESH,
        )

    def arrive(chip, h, s):
        hop(ACROSS, chip, h, s).wait_recv()

    def arrive_pair(chip, h, s):
        piece = gathered.at[chip, h, 1 - core, pl.ds(s * span, span)]
        pltpu.make_async_remote_copy(
            src_ref=piece,
            dst_ref=piece,
            send_sem=send_sem.at[PARTNER, chip, h, s],
            recv_sem=pair_recv.at[chip, h, s],
            device_id=targets[PARTNER],
            device_id_type=MESH,
        ).wait_recv()

    def start(route, chip, h, s):
        hop(route, chip, h, s).start()

    def finish(route, chip, h, s):
        hop(route, chip, h, s).wait_send()

    def own_line(act):
        chip = z * 2 + x
        for s in range(PARTS):
            pl.when(has_up)(lambda: act(UP, chip, group, s))
            pl.when(has_down)(lambda: act(DOWN, chip, group, s))
            act(ACROSS, chip, group, s)

    def own_rest(act):
        for s in range(PARTS):
            act(ACROSS, z * 2 + x, 1 - group, s)

    def own_pair(act):
        for h in range(2):
            for s in range(PARTS):
                act(PARTNER, z * 2 + x, h, s)

    def relay(h, s, act):
        chip = z * 2 + 1 - x
        pl.when(mate > z)(lambda: act(UP, chip, h, s))
        pl.when(mate < z)(lambda: act(DOWN, chip, h, s))

    def at_distance(distance, do):
        for sign in (-1, 1):
            plane = z + sign * distance
            exists = plane >= 0 if sign < 0 else plane < planes
            pl.when(exists)(functools.partial(do, plane, sign))

    def line_step(distance, first, act):
        for s in range(PARTS):

            def do(plane, sign):
                chip = plane * 2 + x
                if first:
                    arrive(chip, group, s)
                if sign < 0:
                    pl.when(has_up)(lambda: act(UP, chip, group, s))
                else:
                    pl.when(has_down)(lambda: act(DOWN, chip, group, s))
                act(OVER, chip, group, s)
                if s < RELAYED:
                    pl.when(plane != mate)(lambda: act(ACROSS, chip, group, s))
                else:
                    act(ACROSS, chip, group, s)
                act(PARTNER, chip, group, s)

            at_distance(distance, do)

    def across_own(first, act):
        for s in range(PARTS):
            if first:
                arrive(z * 2 + 1 - x, group, s)
            act(PARTNER, z * 2 + 1 - x, group, s)

    def relay_own(act):
        for s in range(RELAYED):
            relay(group, s, act)

    def across_rest(first, act):
        for s in range(PARTS):
            if first:
                arrive(z * 2 + 1 - x, 1 - group, s)
            if s >= CORNER_OVER:
                relay(1 - group, s, act)
            act(PARTNER, z * 2 + 1 - x, 1 - group, s)

    def near_step(distance, first, act):
        for s in range(PARTS):

            def do(plane, sign):
                if first:
                    arrive(plane * 2 + x, 1 - group, s)
                act(PARTNER, plane * 2 + x, 1 - group, s)

            at_distance(distance, do)

    def far_piece(chip, s, over, first, act):
        if first:
            arrive(chip, group, s)
        if over:
            act(OVER, chip, group, s)
        act(PARTNER, chip, group, s)

    def far_step(distance, first, act):
        for s in range(PARTS):

            def do(plane, sign):
                pl.when(plane != mate)(
                    lambda: far_piece(plane * 2 + 1 - x, s, True, first, act)
                )

            at_distance(distance, do)

    def mate_step(first, act):
        for s in range(PARTS):
            far_piece(mate * 2 + 1 - x, s, s < CORNER_OVER, first, act)

    def corner_step(distance, first, act):
        def do(plane, sign):
            chip = plane * 2 + 1 - x
            for s in range(PARTS):
                if first:
                    arrive(chip, 1 - group, s)
                act(PARTNER, chip, 1 - group, s)
            if first:
                project(chip)

        at_distance(distance, do)

    def attend(slot):
        def one_head(head, carry):
            lanes = pl.ds(pl.multiple_of(head * head_dim, head_dim), head_dim)
            query = held_queries[slot, :, lanes]
            scores = [
                lax.dot_general(
                    query,
                    ext_keys[places_ref[slot, j], :, lanes],
                    NT,
                    preferred_element_type=jnp.float32,
                )
                * (1.0 / math.sqrt(head_dim))
                + bias_ref[slot, j]
                for j in range(3)
            ]
            row_max = jnp.max(
                jnp.maximum(jnp.maximum(scores[0], scores[1]), scores[2]), axis=-1, keepdims=True
            )
            raw = [jnp.exp(s - row_max) for s in scores]
            denominator = jnp.sum(raw[0] + raw[1] + raw[2], axis=-1, keepdims=True)
            summed = sum(
                jnp.dot(
                    raw[j].astype(jnp.bfloat16),
                    ext_values[places_ref[slot, j], :, lanes],
                    preferred_element_type=jnp.float32,
                )
                for j in range(3)
            )
            scaled = summed / denominator * gates_ref[slot, :, lanes]
            attended[pl.ds(slot * rows, rows), lanes] = scaled.astype(jnp.bfloat16)
            return carry

        lax.fori_loop(0, HEADS, one_head, 0, unroll=4)

    def project(chip):
        for h in range(2):
            for s in range(PARTS):
                arrive_pair(chip, h, s)
        columns = 2 * gathered.shape[3]
        total = sum(
            lax.dot_general(
                attended[:, h * half : (h + 1) * half],
                gathered[chip, h].reshape(columns, half),
                NT,
                preferred_element_type=jnp.float32,
            )
            for h in range(2)
        )
        out_ref[:, pl.ds(pl.multiple_of(chip * columns, columns), columns)] = total.astype(
            out_ref.dtype
        )

    for load in loads[:2]:
        load.wait()
    edge = jnp.logical_or(z == 0, z == planes - 1)
    inner = jnp.logical_not(edge)
    own_line(start)
    for copy in halos:
        copy.start()
    own_pair(start)
    line_step(1, True, start)
    across_own(True, start)
    for load in loads[2:]:
        load.wait()
    for distance in range(2, planes):
        line_step(distance, True, start)
        if distance == 2:
            pl.when(inner)(lambda: own_rest(start))
            relay_own(start)
    pl.when(edge)(lambda: own_rest(start))
    if planes == 2:
        relay_own(start)
    for copy in halos:
        copy.wait_recv()
    attend(0)
    for distance in range(1, planes):
        near_step(distance, True, start)
        far_step(distance, True, start)
        if distance < slots:
            attend(distance)
    for slot in range(planes, slots):
        attend(slot)

    def near_unit(plane, carry):
        project(plane * 2 + x)
        return carry

    lax.fori_loop(0, planes, near_unit, 0)
    mate_step(True, start)
    across_rest(True, start)
    project(z * 2 + 1 - x)
    for distance in (*range(2, planes), 1):
        corner_step(distance, True, start)

    own_line(finish)
    own_rest(finish)
    own_pair(finish)
    across_own(False, finish)
    relay_own(finish)
    across_rest(False, finish)
    mate_step(False, finish)
    for distance in range(1, planes):
        line_step(distance, False, finish)
        near_step(distance, False, finish)
        far_step(distance, False, finish)
        corner_step(distance, False, finish)
    for copy in halos:
        copy.wait_send()


def fits(mesh):
    return mesh.shape["groups"] == 2 and mesh.shape["dp"] in (8, 16)


def on_device_fused(mesh, queries, keys, values, counts, neighbours, gate_table, step, out_weight):
    slots, rows, channels = queries.shape
    planes = mesh.shape["dp"] // 4
    columns = out_weight.shape[1]
    if 2 * columns % 128 or columns % (16 * PARTS):
        return on_device(queries, keys, values, counts, neighbours, gate_table, step, out_weight)
    sentinel = slots + 2 * HALO
    tail_start = jnp.maximum(counts[0] - HALO, 0)
    tail_keys = lax.dynamic_slice_in_dim(keys, tail_start, HALO, 0)
    tail_values = lax.dynamic_slice_in_dim(values, tail_start, HALO, 0)
    half = channels // 2
    weight = jnp.transpose(out_weight.reshape(2, half, columns), (0, 2, 1))
    gate_row = lax.dynamic_index_in_dim(gate_table, step[0], 0, keepdims=False)
    live = (jnp.arange(slots) < counts[0]).astype(jnp.float32)
    gates = live[:, None, None] * gate_row[None, None, :]
    bias = jnp.where(neighbours == sentinel, masked_score, 0.0).astype(jnp.float32)
    bias = jnp.broadcast_to(bias[:, :, None, None], (slots, neighbours.shape[1], 1, rows))
    places = jnp.minimum(neighbours, sentinel - 1)
    chips = planes * 2
    anywhere = pl.BlockSpec(memory_space=pl.ANY)
    vmem = pl.BlockSpec(memory_space=pltpu.VMEM)
    out = pl.pallas_call(
        functools.partial(fused, planes),
        out_shape=jax.ShapeDtypeStruct((slots * rows, chips * 2 * columns), jnp.bfloat16),
        in_specs=[anywhere] * 6 + [vmem, vmem, pl.BlockSpec(memory_space=pltpu.SMEM)],
        out_specs=vmem,
        scratch_shapes=[
            pltpu.VMEM((sentinel, rows, channels), jnp.bfloat16),
            pltpu.VMEM((sentinel, rows, channels), jnp.bfloat16),
            pltpu.VMEM((slots, rows, channels), jnp.bfloat16),
            pltpu.VMEM((slots * rows, channels), jnp.bfloat16),
            pltpu.VMEM((chips, 2, 2, columns, half), jnp.bfloat16),
            pltpu.SemaphoreType.DMA((5,)),
            pltpu.SemaphoreType.DMA((4,)),
            pltpu.SemaphoreType.DMA((4,)),
            pltpu.SemaphoreType.DMA((5, chips, 2, PARTS)),
            pltpu.SemaphoreType.DMA((chips, 2, PARTS)),
            pltpu.SemaphoreType.DMA((chips, 2, PARTS)),
        ],
        compiler_params=pltpu.CompilerParams(
            collective_id=0, has_side_effects=True, vmem_limit_bytes=60 * 2**20
        ),
        name="fused",
    )(keys, values, queries, tail_keys, tail_values, weight, gates, bias, places)
    return out.reshape(slots, rows, -1)


def solution(mesh):
    placed = (
        P(("groups", "dp"), None, None),
        P(("groups", "dp"), None, None),
        P(("groups", "dp"), None, None),
        P(("groups", "dp")),
        P(("groups", "dp"), None),
        P(),
        P(),
        P(None, "dp"),
    )
    return jax.shard_map(
        functools.partial(on_device_fused, mesh) if fits(mesh) else on_device,
        mesh=mesh,
        in_specs=placed,
        out_specs=P(("groups", "dp"), None, None),
        check_vma=False,
    )
```
